128 devices in a mesh: space: 32 (over x, y, core), head: 4 (over z).
Axes of the slice: x: 4, y: 4, z: 4, core: 2. Of those that a mesh axis runs over, the one named last changes fastest.
Arguments:
- snapshot: bfloat16 [32768, 1536], P('space'), may hold values from -6 to 6
- norm_gain: float32 [1536], replicated, may hold values from 0.25 to 1.75
- w_query: bfloat16 [1536, 1536], P(None, 'head'), may hold values from -0.15625 to 0.15625
- w_key: bfloat16 [1536, 1536], P(None, 'head'), may hold values from -0.15625 to 0.15625
- w_value: bfloat16 [1536, 1536], P(None, 'head'), may hold values from -0.15625 to 0.15625
- w_out: bfloat16 [1536, 1536], P('head'), may hold values from -0.15625 to 0.15625
- cache_key: bfloat16 [8, 32768, 1536], P(None, 'space', 'head'), may hold values from -420 to 420
- cache_value: bfloat16 [8, 32768, 1536], P(None, 'space', 'head'), may hold values from -6 to 6
- pattern: int32 [256, 8], P('space'), may hold values from 0 to 255, as said below
- counts: int32 [256], P('space'), may hold values from 1 to 8, as said below
Outputs:
- rolled: bfloat16 [32768, 1536], P('space')
The draws below stay inside these ranges and needn't reach their ends.
Inputs may be any that keep to these rules, and one draw needn't show every extreme that they name: `pattern`: each index is a block within 12 blocks of its query block, counted periodically over the 256 blocks; the 8 entries of one query block are distinct. `counts`: loads are uneven; some query block has all 8 slots live.
All inputs are finite; a program needn't handle non-finite values.
Results may differ from the reference program's by a relative error of at most 0.014.
Values may be sent and summed in bfloat16 or wider, within the bound.
A program may use at most 192 MiB of HBM per device.

```python
import jax
import jax.numpy as jnp
from jax import lax

HD = 128
H = 12
D = 1536
BLK = 128
MAXK = 8
FRAMES = 8
STEPS = 2
TOKENS = 32768
NBLK = 256
REACH = 12
N_HEAD = 4


def draw_pattern(key, part):
    row_keys = jax.random.split(key, NBLK)
    orders = jax.vmap(lambda row_key: jax.random.permutation(row_key, 2 * REACH + 1))(row_keys)
    offsets = orders[:, :MAXK].astype(jnp.int32) - REACH
    return ((jnp.arange(NBLK, dtype=jnp.int32)[:, None] + offsets) % NBLK).astype(jnp.int32)


def draw_counts(key, part):
    loads = jax.random.randint(key, (NBLK,), 1, MAXK + 1).astype(jnp.int32)
    picked = jax.random.randint(jax.random.fold_in(key, 7), (), 0, NBLK)
    return loads.at[picked].set(MAXK).astype(jnp.int32)


def draw_cache_key(key, part):
    values = jax.random.truncated_normal(key, -6.0, 6.0, (FRAMES, TOKENS, D), jnp.float32)
    return values.astype(jnp.bfloat16)


def steps_of(own_key, shape, pieces, low, top_value):
    def one(position, blocks):
        draws = jax.random.uniform(jax.random.fold_in(jax.random.fold_in(own_key, 6), position), (blocks,), jnp.float32, low / len(pieces), top_value / len(pieces))
        return jnp.repeat(jnp.exp(draws), shape[position] // blocks).reshape((-1,) + (1,) * (len(shape) - position - 1))

    loudness = one(*pieces[0])
    for cut in pieces[1:]:
        loudness = loudness * one(*cut)
    return loudness


def gaussian(key, shape, scale, reach, shards=(), kind=jnp.bfloat16):
    values = jax.random.normal(key, shape, jnp.float32) * scale
    if len(shards) > 0:
        values = steps_of(key, shape, shards, -0.22, 0.18) * values
    return jnp.clip(values, min=-reach, max=reach).astype(kind)


def setup_inputs(seed: int = 0) -> dict:
    arg_keys = jax.random.split(jax.random.key(seed), 11)
    return {
        "snapshot": gaussian(arg_keys[0], (TOKENS, D), 1.0, 6.0, ((0, 32),)),
        "norm_gain": jnp.clip(1.0 + 0.15 * jax.random.normal(arg_keys[1], (D,), jnp.float32), 0.25, 1.75),
        "w_query": gaussian(arg_keys[2], (D, D), D ** -0.5, 0.15625, ((1, 4),)),
        "w_key": gaussian(arg_keys[3], (D, D), D ** -0.5, 0.15625, ((1, 4),)),
        "w_value": gaussian(arg_keys[4], (D, D), D ** -0.5, 0.15625, ((1, 4),)),
        "w_out": gaussian(arg_keys[5], (D, D), D ** -0.5, 0.15625, ((0, 4),)),
        "cache_key": draw_cache_key(jax.random.fold_in(arg_keys[10], 71), 0),
        "cache_value": gaussian(arg_keys[7], (FRAMES, TOKENS, D), 1.0, 6.0, ((1, 32), (2, 4))),
        "pattern": draw_pattern(jax.random.fold_in(arg_keys[10], 71), 0),
        "counts": draw_counts(jax.random.fold_in(arg_keys[10], 71), 0),
    }


def attend_block(index, queries, key_complete, value_all, past_key, past_value, pattern, counts):
    inv_scale = 1.0 / HD ** 0.5
    block_query = lax.dynamic_slice_in_dim(queries, index * BLK, BLK, 0).astype(jnp.float32).reshape(BLK, H, HD)
    chosen = pattern[index]
    key_blocks = key_complete.reshape(NBLK, BLK, D)[chosen].astype(jnp.float32).reshape(MAXK, BLK, H, HD)
    value_blocks = value_all.reshape(NBLK, BLK, D)[chosen].astype(jnp.float32).reshape(MAXK, BLK, H, HD)
    cached_key = lax.dynamic_slice_in_dim(past_key, index * BLK, BLK, 1).astype(jnp.float32).reshape(FRAMES, BLK, H, HD)
    cached_value = lax.dynamic_slice_in_dim(past_value, index * BLK, BLK, 1).astype(jnp.float32).reshape(FRAMES, BLK, H, HD)
    spatial = jnp.einsum('qhd,jkhd->hqjk', block_query, key_blocks) * inv_scale
    live_slot = jnp.arange(MAXK) < counts[index]
    spatial = jnp.where(live_slot[None, None, :, None], spatial, jnp.float32(-1e+30))
    temporal = jnp.einsum('qhd,fqhd->hqf', block_query, cached_key) * inv_scale
    top_score = jnp.maximum(spatial.max(axis=(2, 3)), temporal.max(axis=2))
    spatial_exponent = jnp.exp(spatial - top_score[:, :, None, None])
    temporal_exp = jnp.exp(temporal - top_score[:, :, None])
    total = spatial_exponent.sum(axis=(2, 3)) + temporal_exp.sum(axis=2)
    spatial_attention_weight = (spatial_exponent / total[:, :, None, None]).astype(jnp.bfloat16).astype(jnp.float32)
    temporal_weight = (temporal_exp / total[:, :, None]).astype(jnp.bfloat16).astype(jnp.float32)
    mixed = jnp.einsum('hqjk,jkhd->qhd', spatial_attention_weight, value_blocks)
    mixed = mixed + jnp.einsum('hqf,fqhd->qhd', temporal_weight, cached_value)
    return mixed.reshape(BLK, D).astype(jnp.bfloat16)

def reference(snapshot, norm_gain, w_query, w_key, w_value, w_out, cache_key, cache_value, pattern, counts):
    state = snapshot
    past_key, past_value = (cache_key, cache_value)
    group_width = D // N_HEAD
    for rollout in range(STEPS):
        state_wide = state.astype(jnp.float32)
        meansq = lax.optimization_barrier(jnp.mean(state_wide * state_wide, axis=-1, keepdims=True))
        normed = (state_wide * lax.rsqrt(meansq + 1e-05) * norm_gain).astype(jnp.bfloat16)
        queries = jnp.dot(normed, w_query, preferred_element_type=jnp.float32).astype(jnp.bfloat16)
        key_new = jnp.dot(normed, w_key, preferred_element_type=jnp.float32).astype(jnp.bfloat16)
        value_new = jnp.dot(normed, w_value, preferred_element_type=jnp.float32).astype(jnp.bfloat16)
        attended_output = lax.map(lambda index: attend_block(index, queries, key_new, value_new, past_key, past_value, pattern, counts), jnp.arange(NBLK, dtype=jnp.int32))
        attended_output = attended_output.reshape(TOKENS, D)
        update = jnp.zeros((TOKENS, D), jnp.float32)
        for group in range(N_HEAD):
            partial_term = jnp.dot(attended_output[:, group * group_width:(group + 1) * group_width], w_out[group * group_width:(group + 1) * group_width], preferred_element_type=jnp.float32)
            rounded = lax.optimization_barrier(partial_term.astype(jnp.bfloat16))
            update = update + rounded.astype(jnp.float32)
        state = (state_wide + update).astype(jnp.bfloat16)
        if rollout + 1 < STEPS:
            past_key = jnp.concatenate([past_key[1:], key_new[None]], axis=0)
            past_value = jnp.concatenate([past_value[1:], value_new[None]], axis=0)
    return state
```

```python
import functools
import math

import jax
import jax.numpy as jnp
from jax import lax
from jax.experimental import pallas as pl
from jax.experimental.pallas import tpu as pltpu
from jax.sharding import PartitionSpec as P

HD = 128
BLK = 128
MAXK = 8
FRAMES = 8
STEPS = 2
HALO = 12
QBLK = 2
NQ = 4
EPS = 1e-05
MASKED = -1e30
MESH = pl.DeviceIdType.MESH
F32 = jnp.float32
BF16 = jnp.bfloat16
SCALE2 = math.log2(math.e) / math.sqrt(HD)
NORM_ROWS = 32
TIME_ROWS = 32


def kernel(
    n_space, n_head,
    pattern, counts, snapshot, gain, w_query, w_key, w_value, w_out, cache_key, cache_value,
    rolled,
    state, wqkv, wout, ckey, cvalue, kv0, kv1, far, att, queries, normed, top_t, sum_t, acc_t,
    in_sem, w_sem, cache_sem, out_sem,
    near_s, near_r, chip_s, chip_r, far_s, far_r, rel_s, rel_r, ag_s, ag_r, fw_s, fw_r,
    wd_s, wd_r, wf_s, wf_r, wc_s, wc_r,
):
    kv = (kv0, kv1)
    rows, width = state.shape
    lw = w_query.shape[1]
    heads = lw // HD
    blocks = rows // BLK
    total_blocks = blocks * n_space
    qrows = QBLK * BLK
    window = kv0.shape[0]

    space = lax.axis_index("space")
    z = lax.axis_index("head")
    core = lax.rem(space, 2)

    def wrap(s):
        return lax.rem(s + n_space, n_space)

    up = (space, lax.rem(z + 1, n_head))
    down = (space, lax.rem(z + n_head - 1, n_head))
    partner = (space + 1 - 2 * core, z)
    near_dev = (wrap(space - 1 + 2 * core), z)
    far_dev = (wrap(space + 2 - 4 * core), z)
    far_src = (wrap(space - 2 + 4 * core), z)
    z_up = lax.rem(z + 1, n_head)
    z_down = lax.rem(z + n_head - 1, n_head)

    def first_block(q, c):
        return (1 - c) * (blocks - QBLK - QBLK * q) + c * QBLK * q

    def col(group):
        return pl.ds(pl.multiple_of(group * lw, 128), lw)

    def rcopy(src, dst, ssem, rsem, dev):
        return pltpu.make_async_remote_copy(
            src_ref=src, dst_ref=dst, send_sem=ssem, recv_sem=rsem, device_id=dev, device_id_type=MESH
        )

    def near_copy(t, q):
        b = first_block(q, core)
        return rcopy(
            kv[t].at[pl.ds(HALO + b, QBLK)],
            kv[t].at[pl.ds(20 - 16 * core + b, QBLK)],
            near_s.at[t, q], near_r.at[t, q], near_dev,
        )

    def chip_copy(t, q):
        b = first_block(q, core)
        return rcopy(
            kv[t].at[pl.ds(HALO + b, QBLK)],
            kv[t].at[pl.ds(4 + 16 * core + b, QBLK)],
            chip_s.at[t, q], chip_r.at[t, q], partner,
        )

    def far_copy(t, q):
        b = first_block(q, core)
        return rcopy(
            kv[t].at[pl.ds(HALO + b, QBLK)],
            far.at[t, pl.ds(b - 4 * (1 - core), QBLK)],
            far_s.at[t, q], far_r.at[t, q], far_dev,
        )

    def relay_copy(t, q):
        w = 4 + 16 * core + first_block(q, 1 - core)
        return rcopy(
            kv[t].at[pl.ds(w, QBLK)],
            kv[t].at[pl.ds(w - 8 + 16 * core, QBLK)],
            rel_s.at[t, q - 2], rel_r.at[t, q - 2], partner,
        )

    def gather_copy(t, q, d):
        r = pl.multiple_of(first_block(q, core) * BLK, BLK)
        part = att.at[t, pl.ds(r, qrows), col(z)]
        return rcopy(part, part, ag_s.at[t, q, d], ag_r.at[t, q, d], up if d == 0 else down)

    def forward_copy(t, q, d):
        r = pl.multiple_of(first_block(q, core) * BLK + d * (qrows // 2), BLK)
        part = att.at[t, pl.ds(r, qrows // 2), col(z_down if d == 0 else z_up)]
        return rcopy(part, part, fw_s.at[t, q, d], fw_r.at[t, q, d], up if d == 0 else down)

    half = lw // 2

    def w_rows(group, offset, count):
        return wout.at[pl.ds(pl.multiple_of(group * lw + offset, 32), count), :]

    def w_copy(d):
        part = w_rows(z, half * core, half)
        return rcopy(part, part, wd_s.at[d], wd_r.at[d], up if d == 0 else down)

    def w_forward(d):
        part = w_rows(z_down if d == 0 else z_up, half * core + d * (half // 2), half // 2)
        return rcopy(part, part, wf_s.at[d], wf_r.at[d], up if d == 0 else down)

    def w_chip(k):
        part = w_rows(lax.rem(z + 1 + k, n_head), half * core, half)
        return rcopy(part, part, wc_s.at[k], wc_r.at[k], partner)

    def in_copy(q):
        r = pl.multiple_of(first_block(q, core) * BLK, BLK)
        return pltpu.make_async_copy(
            snapshot.at[pl.ds(r, qrows), :], state.at[pl.ds(r, qrows), :], in_sem.at[q]
        )

    def out_copy(q):
        r = pl.multiple_of(first_block(q, core) * BLK, BLK)
        return pltpu.make_async_copy(
            state.at[pl.ds(r, qrows), :], rolled.at[pl.ds(r, qrows), :], out_sem.at[q]
        )

    weight_copies = [
        pltpu.make_async_copy(ref, wqkv.at[:, pl.ds(i * lw, lw)], w_sem.at[i])
        for i, ref in enumerate((w_query, w_key, w_value))
    ]
    w_out_copy = pltpu.make_async_copy(w_out, w_rows(z, 0, lw), w_sem.at[3])
    cache_copies = [
        pltpu.make_async_copy(cache_key, ckey, cache_sem.at[0]),
        pltpu.make_async_copy(cache_value, cvalue, cache_sem.at[1]),
    ]

    def qkv(t, q):
        b = first_block(q, core)
        r0 = b * BLK

        def norm_rows(i, _):
            r = pl.multiple_of(r0 + i * NORM_ROWS, NORM_ROWS)
            wide = state[pl.ds(r, NORM_ROWS), :].astype(F32)
            meansq = jnp.mean(wide * wide, axis=-1, keepdims=True)
            normed[pl.ds(pl.multiple_of(i * NORM_ROWS, NORM_ROWS), NORM_ROWS), :] = (
                wide * lax.rsqrt(meansq + EPS) * gain[...]
            ).astype(BF16)
            return 0

        lax.fori_loop(0, qrows // NORM_ROWS, norm_rows, 0)
        for i in range(2):
            out = jnp.dot(
                normed[...], wqkv[:, lw * (1 + i) : lw * (2 + i)], preferred_element_type=F32
            ).astype(BF16)
            for k in range(QBLK):
                kv[t][HALO + b + k, i] = out[k * BLK : (k + 1) * BLK]
        return r0

    def qkv_queries(q):
        r0 = pl.multiple_of(first_block(q, core) * BLK, BLK)
        queries[pl.ds(r0, qrows), :] = jnp.dot(
            normed[...], wqkv[:, :lw], preferred_element_type=F32
        ).astype(BF16)

    def temporal(t, r, h):
        lanes = slice(h * HD, (h + 1) * HD)
        at = pl.ds(r, TIME_ROWS)
        query = queries[at, lanes].astype(F32)
        b = lax.div(r, BLK)
        inner = pl.ds(pl.multiple_of(lax.rem(r, BLK), TIME_ROWS), TIME_ROWS)
        frames = range(t, FRAMES)
        keys = [ckey[f, at, lanes] for f in frames]
        keys += [kv0[HALO + b, 0, inner, lanes]] * t
        scores = [jnp.sum(query * k.astype(F32), axis=-1, keepdims=True) for k in keys]
        top = functools.reduce(jnp.maximum, scores)
        exps = [jnp.exp2((s - top) * SCALE2) for s in scores]
        values = [cvalue[f, at, lanes] for f in frames]
        values += [kv0[HALO + b, 1, inner, lanes]] * t
        acc = functools.reduce(jnp.add, [e * v.astype(F32) for e, v in zip(exps, values)])
        top_t[at, lanes] = jnp.broadcast_to(top, (TIME_ROWS, HD))
        sum_t[at, lanes] = jnp.broadcast_to(functools.reduce(jnp.add, exps), (TIME_ROWS, HD))
        acc_t[at, lanes] = acc

    def temporal_quarter(t, q):
        r0 = first_block(q, core) * BLK

        def body(i, _):
            r = pl.multiple_of(r0 + i * TIME_ROWS, TIME_ROWS)
            for h in range(heads):
                temporal(t, r, h)
            return 0

        lax.fori_loop(0, qrows // TIME_ROWS, body, 0)

    def attend(t, b):
        r = pl.ds(pl.multiple_of(b * BLK, BLK), BLK)
        live = counts[b]
        where, bias = [], []
        for j in range(MAXK):
            rel = pattern[b, j] - (space * blocks + b) + total_blocks // 2
            rel = jnp.bitwise_and(rel, total_blocks - 1) - total_blocks // 2
            where.append(jnp.clip(HALO + b + rel, 0, window - 1))
            bias.append(jnp.where(j < live, jnp.float32(0.0), jnp.float32(MASKED)))
        for h in range(heads):
            lanes = slice(h * HD, (h + 1) * HD)
            query = queries[r, lanes]
            scores = []
            for j in range(0, MAXK, 2):
                pair = jnp.concatenate([kv[t][where[j + i], 0, :, lanes] for i in range(2)], axis=0)
                s = lax.dot_general(
                    query, pair, (((1,), (1,)), ((), ())), preferred_element_type=F32
                )
                scores += [s[:, i * BLK : (i + 1) * BLK] + bias[j + i] for i in range(2)]
            top = jnp.max(functools.reduce(jnp.maximum, scores), axis=-1, keepdims=True)
            old = top_t[r, lanes]
            top = jnp.maximum(old, jnp.broadcast_to(top, (BLK, HD)))
            keep = jnp.exp2((old - top) * SCALE2)
            exps = [jnp.exp2((s - top) * SCALE2) for s in scores]
            total = jnp.sum(functools.reduce(jnp.add, exps), axis=-1, keepdims=True)
            acc = acc_t[r, lanes] * keep
            for j in range(0, MAXK, 2):
                pair = jnp.concatenate([kv[t][where[j + i], 1, :, lanes] for i in range(2)], axis=0)
                weights = jnp.concatenate([exps[j + i].astype(BF16) for i in range(2)], axis=1)
                acc = acc + jnp.dot(weights, pair, preferred_element_type=F32)
            total = sum_t[r, lanes] * keep + total
            out = pl.ds(pl.multiple_of(z * lw + h * HD, HD), HD)
            att[t, r, out] = (acc / total).astype(BF16)

    n_cols = 512

    def update(t, q):
        r = pl.ds(pl.multiple_of(first_block(q, core) * BLK, BLK), qrows)
        for n in range(0, width, n_cols):
            u = jnp.dot(att[t, r, :], wout[:, n : n + n_cols], preferred_element_type=F32)
            state[r, n : n + n_cols] = (state[r, n : n + n_cols].astype(F32) + u).astype(BF16)

    for i in range(NQ):
        in_copy(NQ - 1 - i).start()
    for copy in (weight_copies[1], weight_copies[2], weight_copies[0], w_out_copy):
        copy.start()
    for copy in cache_copies:
        copy.start()

    barrier = pltpu.get_barrier_semaphore()
    for dev in (up, down, partner, near_dev, far_dev, far_src):
        pl.semaphore_signal(barrier, inc=1, device_id=dev, device_id_type=MESH)
    pl.semaphore_wait(barrier, 6)

    weight_copies[1].wait()
    weight_copies[2].wait()
    weight_copies[0].wait()

    def first_qkv(i, _):
        q = NQ - 1 - i
        in_copy(q).wait()
        qkv(0, q)
        near_copy(0, q).start()
        chip_copy(0, q).start()
        qkv_queries(q)

        @pl.when(i == 0)
        def _():
            w_out_copy.wait()
            for d in range(2):
                w_copy(d).start()

        return 0

    lax.fori_loop(0, NQ, first_qkv, 0)
    for copy in cache_copies:
        copy.wait()

    def first_temporal(q, _):
        temporal_quarter(0, q)
        return 0

    lax.fori_loop(0, NQ, first_temporal, 0)

    for d in range(2):
        w_copy(d).wait_recv()
        w_forward(d).start()
    w_chip(0).start()
    w_chip(2).start()

    def near_wait(t):
        for q in (3, 2):
            near_copy(t, q).wait_recv()
            relay_copy(t, q).start()
        for q in (1, 0):
            near_copy(t, q).wait_recv()

    def far_wait(t):
        for q in range(2):
            far_copy(t, q).wait_recv()
        for i in range(4):
            kv[t][28 * core + i] = far[t, i]

    near_wait(0)
    for q in (0, 1):
        far_copy(0, q).start()
    for d in range(2):
        w_forward(d).wait_recv()
    w_chip(1).start()

    for t in range(STEPS):
        if t > 0:
            near_wait(t)
        for q in range(NQ):
            chip_copy(t, q).wait_recv()
        for q in (3, 2):
            relay_copy(t, q).wait_recv()

        def forward(t, q):
            for d in range(2):
                gather_copy(t, q, d).wait_recv()
                forward_copy(t, q, d).start()

        def attend_quarter(q, _, t=t):
            @pl.when(q == 2)
            def _():
                far_wait(t)

            b = first_block(q, core)

            def body(k, _):
                attend(t, b + k)
                return 0

            lax.fori_loop(0, QBLK, body, 0)
            for d in range(2):
                gather_copy(t, q, d).start()

            @pl.when(q > 0)
            def _():
                forward(t, q - 1)

            return 0

        lax.fori_loop(0, NQ, attend_quarter, 0)

        def finish_quarter(q, _, t=t):
            @pl.when(q == 0)
            def _():
                forward(t, NQ - 1)

            for d in range(2):
                forward_copy(t, q, d).wait_recv()
            if t == 0:

                @pl.when(q == 0)
                def _():
                    for k in range(3):
                        w_chip(k).wait_recv()

            update(t, q)
            if t + 1 < STEPS:
                qkv(t + 1, q)
                near_copy(t + 1, q).start()
                chip_copy(t + 1, q).start()

                @pl.when(q < 2)
                def _():
                    far_copy(t + 1, q).start()

                qkv_queries(q)
                temporal_quarter(t + 1, q)
            else:
                out_copy(q).start()
            return 0

        lax.fori_loop(0, NQ, finish_quarter, 0)

    for q in range(NQ):
        out_copy(q).wait()
    for t in range(STEPS):
        for q in range(NQ):
            near_copy(t, q).wait_send()
            chip_copy(t, q).wait_send()
            for d in range(2):
                gather_copy(t, q, d).wait_send()
                forward_copy(t, q, d).wait_send()
        for q in range(2):
            far_copy(t, q).wait_send()
            relay_copy(t, q + 2).wait_send()
    for d in range(2):
        w_copy(d).wait_send()
        w_forward(d).wait_send()
    for k in range(3):
        w_chip(k).wait_send()


def on_device(
    n_space, n_head,
    snapshot, norm_gain, w_query, w_key, w_value, w_out, cache_key, cache_value, pattern, counts,
):
    rows, width = snapshot.shape
    lw = w_query.shape[1]
    blocks = rows // BLK
    any_spec = pl.BlockSpec(memory_space=pl.ANY)
    smem = pl.BlockSpec(memory_space=pltpu.SMEM)
    window = blocks + 2 * HALO
    dma = pltpu.SemaphoreType.DMA
    return pl.pallas_call(
        functools.partial(kernel, n_space, n_head),
        out_shape=jax.ShapeDtypeStruct((rows, width), BF16),
        in_specs=[smem, smem, any_spec, pl.BlockSpec(memory_space=pltpu.VMEM)] + [any_spec] * 6,
        out_specs=any_spec,
        scratch_shapes=[
            pltpu.VMEM((rows, width), BF16),
            pltpu.VMEM((width, 3 * lw), BF16),
            pltpu.VMEM((width, width), BF16),
            pltpu.VMEM((FRAMES, rows, lw), BF16),
            pltpu.VMEM((FRAMES, rows, lw), BF16),
            pltpu.VMEM((window, 2, BLK, lw), BF16),
            pltpu.VMEM((window, 2, BLK, lw), BF16),
            pltpu.VMEM((STEPS, 4, 2, BLK, lw), BF16),
            pltpu.VMEM((STEPS, rows, width), BF16),
            pltpu.VMEM((rows, lw), BF16),
            pltpu.VMEM((QBLK * BLK, width), BF16),
            pltpu.VMEM((rows, lw), F32),
            pltpu.VMEM((rows, lw), F32),
            pltpu.VMEM((rows, lw), F32),
            dma((NQ,)), dma((4,)), dma((2,)), dma((NQ,)),
            dma((STEPS, NQ)), dma((STEPS, NQ)),
            dma((STEPS, NQ)), dma((STEPS, NQ)),
            dma((STEPS, 2)), dma((STEPS, 2)),
            dma((STEPS, 2)), dma((STEPS, 2)),
            dma((STEPS, NQ, 2)), dma((STEPS, NQ, 2)),
            dma((STEPS, NQ, 2)), dma((STEPS, NQ, 2)),
            dma((2,)), dma((2,)), dma((2,)), dma((2,)), dma((3,)), dma((3,)),
        ],
        compiler_params=pltpu.CompilerParams(
            collective_id=0, has_side_effects=True, vmem_limit_bytes=60 * 1024 * 1024
        ),
        name="rollout",
    )(
        pattern, counts, snapshot, norm_gain.reshape(1, width),
        w_query, w_key, w_value, w_out, cache_key, cache_value,
    )


def solution(mesh):
    placed = (
        P("space", None),
        P(),
        P(None, "head"),
        P(None, "head"),
        P(None, "head"),
        P("head", None),
        P(None, "space", "head"),
        P(None, "space", "head"),
        P("space", None),
        P("space"),
    )
    body = functools.partial(on_device, mesh.shape["space"], mesh.shape["head"])
    return jax.shard_map(
        body, mesh=mesh, in_specs=placed, out_specs=P("space", None), check_vma=False
    )
```

```python
import functools
import math

import jax
import jax.numpy as jnp
from jax import lax
from jax.experimental import pallas as pl
from jax.experimental.pallas import tpu as pltpu
from jax.sharding import PartitionSpec as P

HD = 128
BLK = 128
MAXK = 8
FRAMES = 8
STEPS = 2
HALO = 12
QBLK = 2
NQ = 4
EPS = 1e-05
MASKED = -1e30
MESH = pl.DeviceIdType.MESH
F32 = jnp.float32
BF16 = jnp.bfloat16
SCALE2 = math.log2(math.e) / math.sqrt(HD)
NORM_ROWS = 64
COLS = 512
TIME_ROWS = 32


def kernel(
    n_space, n_head,
    pattern, counts, snapshot, gain, w_query, w_key, w_value, w_out, cache_key, cache_value,
    state,
    wqkv, wout, ckey, cvalue, kv0, kv1, late, att, queries, normed, top_t, sum_t, acc_t,
    in_sem, w_sem, cache_sem,
    near_s, near_r, chip_s, chip_r, far_s, far_r, rel_s, rel_r, ag_s, ag_r, fw_s, fw_r,
    wd_s, wd_r, wf_s, wf_r, wc_s, wc_r,
):
    kv = (kv0, kv1)
    rows, width = state.shape
    lw = w_query.shape[1]
    heads = lw // HD
    blocks = rows // BLK
    total_blocks = blocks * n_space
    qrows = QBLK * BLK
    window = kv0.shape[0]

    space = lax.axis_index("space")
    z = lax.axis_index("head")
    core = lax.rem(space, 2)

    def wrap(s):
        return lax.rem(s + n_space, n_space)

    up = (space, lax.rem(z + 1, n_head))
    down = (space, lax.rem(z + n_head - 1, n_head))
    partner = (space + 1 - 2 * core, z)
    near_dev = (wrap(space - 1 + 2 * core), z)
    far_dev = (wrap(space + 2 - 4 * core), z)
    far_src = (wrap(space - 2 + 4 * core), z)
    z_up = lax.rem(z + 1, n_head)
    z_down = lax.rem(z + n_head - 1, n_head)

    def first_block(q, c):
        return (1 - c) * (blocks - QBLK - QBLK * q) + c * QBLK * q

    def col(group):
        return pl.ds(pl.multiple_of(group * lw, 128), lw)

    def rcopy(src, dst, ssem, rsem, dev):
        return pltpu.make_async_remote_copy(
            src_ref=src, dst_ref=dst, send_sem=ssem, recv_sem=rsem, device_id=dev, device_id_type=MESH
        )

    def near_window(q):
        return 4 + 16 * core + first_block(q, 1 - core)

    def near_copy(t, q, last=False):
        b = first_block(q, core)
        return rcopy(
            kv[t].at[pl.ds(HALO + b, QBLK)],
            late.at[t, 0] if last else kv[t].at[pl.ds(20 - 16 * core + b, QBLK)],
            near_s.at[t, q], near_r.at[t, q], near_dev,
        )

    def near_start(t, q):
        @pl.when(q == 0)
        def _():
            near_copy(t, 0, True).start()

        @pl.when(q > 0)
        def _():
            near_copy(t, q).start()

    def chip_copy(t, q):
        b = first_block(q, core)
        return rcopy(
            kv[t].at[pl.ds(HALO + b, QBLK)],
            kv[t].at[pl.ds(4 + 16 * core + b, QBLK)],
            chip_s.at[t, q], chip_r.at[t, q], partner,
        )

    def far_copy(t, q):
        b = first_block(q, core)
        return rcopy(
            kv[t].at[pl.ds(HALO + b, QBLK)],
            late.at[t, 1 + q],
            far_s.at[t, q], far_r.at[t, q], far_dev,
        )

    def relay_copy(t, q):
        w = near_window(q)
        return rcopy(
            kv[t].at[pl.ds(w, QBLK)],
            kv[t].at[pl.ds(w - 8 + 16 * core, QBLK)],
            rel_s.at[t, q - 2], rel_r.at[t, q - 2], partner,
        )

    def gather_copy(t, q, d):
        r = pl.multiple_of(first_block(q, core) * BLK, BLK)
        part = att.at[t, pl.ds(r, qrows), col(z)]
        return rcopy(part, part, ag_s.at[t, q, d], ag_r.at[t, q, d], up if d == 0 else down)

    def forward_copy(t, q, d):
        r = pl.multiple_of(first_block(q, core) * BLK + d * (qrows // 2), BLK)
        part = att.at[t, pl.ds(r, qrows // 2), col(z_down if d == 0 else z_up)]
        return rcopy(part, part, fw_s.at[t, q, d], fw_r.at[t, q, d], up if d == 0 else down)

    half = lw // 2

    def w_rows(group, offset, count):
        return wout.at[pl.ds(pl.multiple_of(group * lw + offset, 32), count), :]

    def w_copy(d):
        part = w_rows(z, half * core, half)
        return rcopy(part, part, wd_s.at[d], wd_r.at[d], up if d == 0 else down)

    def w_forward(d):
        part = w_rows(z_down if d == 0 else z_up, half * core + d * (half // 2), half // 2)
        return rcopy(part, part, wf_s.at[d], wf_r.at[d], up if d == 0 else down)

    def w_chip(k):
        part = w_rows(lax.rem(z + 1 + k, n_head), half * core, half)
        return rcopy(part, part, wc_s.at[k], wc_r.at[k], partner)

    def in_copy(q):
        r = pl.multiple_of(first_block(q, core) * BLK, BLK)
        return pltpu.make_async_copy(
            snapshot.at[pl.ds(r, qrows), :], state.at[pl.ds(r, qrows), :], in_sem.at[q]
        )

    weight_copies = [
        pltpu.make_async_copy(ref, wqkv.at[:, pl.ds(i * lw, lw)], w_sem.at[i])
        for i, ref in enumerate((w_key, w_value, w_query))
    ]
    w_out_copy = pltpu.make_async_copy(w_out, w_rows(z, 0, lw), w_sem.at[3])
    cache_copies = [
        pltpu.make_async_copy(cache_key, ckey, cache_sem.at[0]),
        pltpu.make_async_copy(cache_value, cvalue, cache_sem.at[1]),
    ]

    def qkv(t, q):
        b = first_block(q, core)
        r0 = b * BLK

        def norm_rows(i, _):
            r = pl.multiple_of(r0 + i * NORM_ROWS, NORM_ROWS)
            wide = state[pl.ds(r, NORM_ROWS), :].astype(F32)
            meansq = jnp.mean(wide * wide, axis=-1, keepdims=True)
            normed[pl.ds(pl.multiple_of(i * NORM_ROWS, NORM_ROWS), NORM_ROWS), :] = (
                wide * lax.rsqrt(meansq + EPS) * gain[...].reshape(1, width)
            ).astype(BF16)
            return 0

        lax.fori_loop(0, qrows // NORM_ROWS, norm_rows, 0)
        for n in range(0, 3 * lw, COLS):
            out = jnp.dot(normed[...], wqkv[:, n : n + COLS], preferred_element_type=F32)
            for c in range(n, min(n + COLS, 3 * lw), HD):
                kind, lane = divmod(c, lw)
                piece = out[:, c - n : c - n + HD].astype(BF16)
                lanes = slice(lane, lane + HD)
                if kind == 2:
                    queries[pl.ds(pl.multiple_of(r0, BLK), qrows), lanes] = piece
                    continue
                for k in range(QBLK):
                    kv[t][HALO + b + k, kind, :, lanes] = piece[k * BLK : (k + 1) * BLK]

    def temporal(t, r, h):
        lanes = slice(h * HD, (h + 1) * HD)
        at = pl.ds(r, TIME_ROWS)
        query = queries[at, lanes].astype(F32)
        b = lax.div(r, BLK)
        inner = pl.ds(pl.multiple_of(lax.rem(r, BLK), TIME_ROWS), TIME_ROWS)
        frames = range(t, FRAMES)
        keys = [ckey[f, at, lanes] for f in frames]
        keys += [kv0[HALO + b, 0, inner, lanes]] * t
        scores = [jnp.sum(query * k.astype(F32), axis=-1, keepdims=True) for k in keys]
        top = functools.reduce(jnp.maximum, scores)
        exps = [jnp.exp2((s - top) * SCALE2) for s in scores]
        values = [cvalue[f, at, lanes] for f in frames]
        values += [kv0[HALO + b, 1, inner, lanes]] * t
        acc = functools.reduce(jnp.add, [e * v.astype(F32) for e, v in zip(exps, values)])
        top_t[at, lanes] = jnp.broadcast_to(top, (TIME_ROWS, HD))
        sum_t[at, lanes] = jnp.broadcast_to(functools.reduce(jnp.add, exps), (TIME_ROWS, HD))
        acc_t[at, lanes] = acc

    def temporal_quarter(t, q):
        r0 = first_block(q, core) * BLK

        def body(i, _):
            r = pl.multiple_of(r0 + i * TIME_ROWS, TIME_ROWS)
            for h in range(heads):
                temporal(t, r, h)
            return 0

        lax.fori_loop(0, qrows // TIME_ROWS, body, 0)

    def attend(t, b):
        r = pl.ds(pl.multiple_of(b * BLK, BLK), BLK)
        live = counts[b]
        where, bias = [], []
        for j in range(MAXK):
            rel = pattern[b, j] - (space * blocks + b) + total_blocks // 2
            rel = jnp.bitwise_and(rel, total_blocks - 1) - total_blocks // 2
            where.append(jnp.clip(HALO + b + rel, 0, window - 1))
            bias.append(jnp.where(j < live, jnp.float32(0.0), jnp.float32(MASKED)))
        for h in range(heads):
            lanes = slice(h * HD, (h + 1) * HD)
            query = queries[r, lanes]
            scores = []
            for j in range(0, MAXK, 2):
                pair = jnp.concatenate([kv[t][where[j + i], 0, :, lanes] for i in range(2)], axis=0)
                s = lax.dot_general(
                    query, pair, (((1,), (1,)), ((), ())), preferred_element_type=F32
                )
                scores += [s[:, i * BLK : (i + 1) * BLK] + bias[j + i] for i in range(2)]
            top = jnp.max(functools.reduce(jnp.maximum, scores), axis=-1, keepdims=True)
            old = top_t[r, lanes]
            top = jnp.maximum(old, jnp.broadcast_to(top, (BLK, HD)))
            keep = jnp.exp2((old - top) * SCALE2)
            exps = [jnp.exp2((s - top) * SCALE2) for s in scores]
            total = jnp.sum(functools.reduce(jnp.add, exps), axis=-1, keepdims=True)
            acc = acc_t[r, lanes] * keep
            for j in range(0, MAXK, 2):
                pair = jnp.concatenate([kv[t][where[j + i], 1, :, lanes] for i in range(2)], axis=0)
                weights = jnp.concatenate([exps[j + i].astype(BF16) for i in range(2)], axis=1)
                acc = acc + jnp.dot(weights, pair, preferred_element_type=F32)
            total = sum_t[r, lanes] * keep + total
            out = pl.ds(pl.multiple_of(z * lw + h * HD, HD), HD)
            att[t, r, out] = (acc / total).astype(BF16)

    def update(t, q):
        r = pl.ds(pl.multiple_of(first_block(q, core) * BLK, BLK), qrows)
        for n in range(0, width, COLS):
            u = jnp.dot(att[t, r, :], wout[:, n : n + COLS], preferred_element_type=F32)
            state[r, n : n + COLS] = (state[r, n : n + COLS].astype(F32) + u).astype(BF16)

    for i in range(NQ):
        in_copy(NQ - 1 - i).start()
    for copy in weight_copies:
        copy.start()
    w_out_copy.start()

    barrier = pltpu.get_barrier_semaphore()
    for dev in (up, down, partner, near_dev, far_dev, far_src):
        pl.semaphore_signal(barrier, inc=1, device_id=dev, device_id_type=MESH)
    pl.semaphore_wait(barrier, 6)

    for copy in weight_copies:
        copy.wait()
    w_out_copy.wait()
    for d in range(2):
        w_copy(d).start()
    for copy in cache_copies:
        copy.start()

    def first_qkv(i, _):
        q = NQ - 1 - i
        in_copy(q).wait()
        qkv(0, q)
        near_start(0, q)
        chip_copy(0, q).start()
        return 0

    lax.fori_loop(0, NQ, first_qkv, 0)
    for copy in cache_copies:
        copy.wait()

    def near_wait(t, q):
        near_copy(t, q).wait_recv()
        if q >= 2:
            relay_copy(t, q).start()

    def land(t, slot, w):
        for i in range(QBLK):
            kv[t][w + i] = late[t, slot, i]

    def far_land(t, q):
        far_copy(t, q).wait_recv()
        b = first_block(q, core)
        land(t, 1 + q, 28 * core + b - 4 * (1 - core))

    def first_temporal(q, _):
        temporal_quarter(0, q)

        @pl.when(q == 2)
        def _():
            for d in range(2):
                w_copy(d).wait_recv()
                w_forward(d).start()
            w_chip(0).start()
            w_chip(2).start()
            for k in (3, 2):
                near_wait(0, k)

        return 0

    lax.fori_loop(0, NQ, first_temporal, 0)

    for t in range(STEPS):
        if t == 0:
            near_wait(t, 1)
            far_copy(t, 0).start()
        else:
            for q in (1, 2, 3):
                near_wait(t, q)
            far_copy(t, 1).start()
        for q in range(NQ):
            chip_copy(t, q).wait_recv()
        for q in (2, 3):
            relay_copy(t, q).wait_recv()

        def forward(t, q):
            for d in range(2):
                gather_copy(t, q, d).wait_recv()
                forward_copy(t, q, d).start()

        def attend_quarter(q, _, t=t):
            @pl.when(q == 1)
            def _():
                near_copy(t, 0, True).wait_recv()
                if t == 0:
                    far_copy(t, 1).start()
                land(t, 0, near_window(0))

            @pl.when(q > 1)
            def _():
                forward(t, q - 2)
                far_land(t, q - 2)

            b = first_block(q, core)

            def body(k, _):
                attend(t, b + k)
                return 0

            lax.fori_loop(0, QBLK, body, 0)
            for d in range(2):
                gather_copy(t, q, d).start()

            if t == 0:

                @pl.when(q == 2)
                def _():
                    for d in range(2):
                        w_forward(d).wait_recv()
                    w_chip(1).start()

            return 0

        lax.fori_loop(0, NQ, attend_quarter, 0)

        def finish_quarter(q, _, t=t):
            @pl.when((q == 1) | (q == 2))
            def _():
                forward(t, q + 1)

            for d in range(2):
                forward_copy(t, q, d).wait_recv()
            if t == 0:

                @pl.when(q == 0)
                def _():
                    for k in range(3):
                        w_chip(k).wait_recv()

            update(t, q)
            if t + 1 < STEPS:
                qkv(t + 1, q)
                near_start(t + 1, q)
                chip_copy(t + 1, q).start()

                @pl.when(q == 0)
                def _():
                    far_copy(t + 1, 0).start()

                temporal_quarter(t + 1, q)
            return 0

        lax.fori_loop(0, NQ, finish_quarter, 0)

    for t in range(STEPS):
        for q in range(NQ):
            near_copy(t, q, q == 0).wait_send()
            chip_copy(t, q).wait_send()
            for d in range(2):
                gather_copy(t, q, d).wait_send()
                forward_copy(t, q, d).wait_send()
        for q in range(2):
            far_copy(t, q).wait_send()
            relay_copy(t, q + 2).wait_send()
    for d in range(2):
        w_copy(d).wait_send()
        w_forward(d).wait_send()
    for k in range(3):
        w_chip(k).wait_send()


def on_device(
    n_space, n_head,
    snapshot, norm_gain, w_query, w_key, w_value, w_out, cache_key, cache_value, pattern, counts,
):
    rows, width = snapshot.shape
    lw = w_query.shape[1]
    blocks = rows // BLK
    any_spec = pl.BlockSpec(memory_space=pl.ANY)
    smem = pl.BlockSpec(memory_space=pltpu.SMEM)
    window = blocks + 2 * HALO
    dma = pltpu.SemaphoreType.DMA
    return pl.pallas_call(
        functools.partial(kernel, n_space, n_head),
        out_shape=pltpu.VMEM((rows, width), BF16),
        in_specs=[smem, smem, any_spec, pl.BlockSpec(memory_space=pltpu.VMEM)] + [any_spec] * 6,
        out_specs=pl.BlockSpec(memory_space=pltpu.VMEM),
        scratch_shapes=[
            pltpu.VMEM((width, 3 * lw), BF16),
            pltpu.VMEM((width, width), BF16),
            pltpu.VMEM((FRAMES, rows, lw), BF16),
            pltpu.VMEM((FRAMES, rows, lw), BF16),
            pltpu.VMEM((window, 2, BLK, lw), BF16),
            pltpu.VMEM((window, 2, BLK, lw), BF16),
            pltpu.VMEM((STEPS, 3, QBLK, 2, BLK, lw), BF16),
            pltpu.VMEM((STEPS, rows, width), BF16),
            pltpu.VMEM((rows, lw), BF16),
            pltpu.VMEM((QBLK * BLK, width), BF16),
            pltpu.VMEM((rows, lw), F32),
            pltpu.VMEM((rows, lw), F32),
            pltpu.VMEM((rows, lw), F32),
            dma((NQ,)), dma((4,)), dma((2,)),
            dma((STEPS, NQ)), dma((STEPS, NQ)),
            dma((STEPS, NQ)), dma((STEPS, NQ)),
            dma((STEPS, 2)), dma((STEPS, 2)),
            dma((STEPS, 2)), dma((STEPS, 2)),
            dma((STEPS, NQ, 2)), dma((STEPS, NQ, 2)),
            dma((STEPS, NQ, 2)), dma((STEPS, NQ, 2)),
            dma((2,)), dma((2,)), dma((2,)), dma((2,)), dma((3,)), dma((3,)),
        ],
        compiler_params=pltpu.CompilerParams(
            collective_id=0, has_side_effects=True, vmem_limit_bytes=56 * 1024 * 1024
        ),
        name="rollout",
    )(
        pattern, counts, snapshot, norm_gain,
        w_query, w_key, w_value, w_out, cache_key, cache_value,
    )


def solution(mesh):
    placed = (
        P("space", None),
        P(),
        P(None, "head"),
        P(None, "head"),
        P(None, "head"),
        P("head", None),
        P(None, "space", "head"),
        P(None, "space", "head"),
        P("space", None),
        P("space"),
    )
    body = functools.partial(on_device, mesh.shape["space"], mesh.shape["head"])
    return jax.shard_map(
        body, mesh=mesh, in_specs=placed, out_specs=P("space", None), check_vma=False
    )
```

```python
import functools
import math

import jax
import jax.numpy as jnp
from jax import lax
from jax.experimental import pallas as pl
from jax.experimental.pallas import tpu as pltpu
from jax.sharding import PartitionSpec as P

HD = 128
BLK = 128
MAXK = 8
FRAMES = 8
STEPS = 2
HALO = 12
FAR = 4
FORWARD_LAG = (2, 2)
FINISH_LAG = (4, 4)
NEAR_LATE = 3
EPS = 1e-05
MASKED = -1e30
MESH = pl.DeviceIdType.MESH
F32 = jnp.float32
BF16 = jnp.bfloat16
SCALE2 = math.log2(math.e) / math.sqrt(HD)
NORM_ROWS = 64
COLS = 512
TIME_ROWS = 32


def kernel(
    n_space, n_head,
    pattern, counts, snapshot, gain, w_query, w_key, w_value, w_out, cache_key, cache_value,
    state,
    wqkv, wout, ckey, cvalue, kv0, kv1, late, att, queries, normed, top_t, sum_t, acc_t, scores, weights,
    in_sem, w_sem, cache_sem,
    near_s, near_r, chip_s, chip_r, far_s, far_r, rel_s, rel_r, ag_s, ag_r, fw_s, fw_r,
    wd_s, wd_r, wf_s, wf_r, wc_s, wc_r,
):
    kv = (kv0, kv1)
    rows, width = state.shape
    lw = w_query.shape[1]
    heads = lw // HD
    blocks = rows // BLK
    total_blocks = blocks * n_space
    window = kv0.shape[0]

    space = lax.axis_index("space")
    z = lax.axis_index("head")
    core = lax.rem(space, 2)

    def wrap(s):
        return lax.rem(s + n_space, n_space)

    up = (space, lax.rem(z + 1, n_head))
    down = (space, lax.rem(z + n_head - 1, n_head))
    partner = (space + 1 - 2 * core, z)
    near_dev = (wrap(space - 1 + 2 * core), z)
    far_dev = (wrap(space + 2 - 4 * core), z)
    far_src = (wrap(space - 2 + 4 * core), z)
    z_up = lax.rem(z + 1, n_head)
    z_down = lax.rem(z + n_head - 1, n_head)

    def block_of(q, c):
        return (1 - c) * (blocks - 1 - q) + c * q

    def rcopy(src, dst, ssem, rsem, dev):
        return pltpu.make_async_remote_copy(
            src_ref=src, dst_ref=dst, send_sem=ssem, recv_sem=rsem, device_id=dev, device_id_type=MESH
        )

    def near_window(q):
        return 4 + 16 * core + block_of(q, 1 - core)

    def near_copy(t, q, last=False):
        b = block_of(q, core)
        return rcopy(
            kv[t].at[HALO + b],
            late.at[t, NEAR_LATE - 1 - q] if last else kv[t].at[20 - 16 * core + b],
            near_s.at[t, q], near_r.at[t, q], near_dev,
        )

    def near_start(t, q):
        @pl.when(q < NEAR_LATE)
        def _():
            near_copy(t, q, True).start()

        @pl.when(q >= NEAR_LATE)
        def _():
            near_copy(t, q).start()

    def chip_copy(t, q):
        b = block_of(q, core)
        return rcopy(
            kv[t].at[HALO + b],
            kv[t].at[4 + 16 * core + b],
            chip_s.at[t, q], chip_r.at[t, q], partner,
        )

    def far_copy(t, q):
        b = block_of(q, core)
        return rcopy(
            kv[t].at[HALO + b],
            late.at[t, NEAR_LATE + q],
            far_s.at[t, q], far_r.at[t, q], far_dev,
        )

    def relay_copy(t, q):
        w = near_window(q)
        return rcopy(
            kv[t].at[w],
            kv[t].at[w - 8 + 16 * core],
            rel_s.at[t, q - FAR], rel_r.at[t, q - FAR], partner,
        )

    def gather_copy(t, q, d):
        r = pl.multiple_of(block_of(q, core) * BLK, BLK)
        part = att.at[t, pl.ds(z * heads, heads), pl.ds(r, BLK), :]
        return rcopy(part, part, ag_s.at[t, q, d], ag_r.at[t, q, d], up if d == 0 else down)

    def forward_copy(t, q, d):
        r = pl.multiple_of(block_of(q, core) * BLK + d * (BLK // 2), BLK // 2)
        source = z_down if d == 0 else z_up
        part = att.at[t, pl.ds(source * heads, heads), pl.ds(r, BLK // 2), :]
        return rcopy(part, part, fw_s.at[t, q, d], fw_r.at[t, q, d], up if d == 0 else down)

    half = lw // 2

    def w_rows(group, offset, count):
        return wout.at[pl.ds(pl.multiple_of(group * lw + offset, 32), count), :]

    def w_copy(d):
        part = w_rows(z, half * core, half)
        return rcopy(part, part, wd_s.at[d], wd_r.at[d], up if d == 0 else down)

    def w_forward(d):
        part = w_rows(z_down if d == 0 else z_up, half * core + d * (half // 2), half // 2)
        return rcopy(part, part, wf_s.at[d], wf_r.at[d], up if d == 0 else down)

    def w_chip(k):
        part = w_rows(lax.rem(z + 1 + k, n_head), half * core, half)
        return rcopy(part, part, wc_s.at[k], wc_r.at[k], partner)

    def in_copy(q):
        r = pl.multiple_of(block_of(q, core) * BLK, BLK)
        return pltpu.make_async_copy(
            snapshot.at[pl.ds(r, BLK), :], state.at[pl.ds(r, BLK), :], in_sem.at[q]
        )

    weight_copies = [
        pltpu.make_async_copy(ref, wqkv.at[:, pl.ds(i * lw, lw)], w_sem.at[i])
        for i, ref in enumerate((w_key, w_value, w_query))
    ]
    w_out_copy = pltpu.make_async_copy(w_out, w_rows(z, 0, lw), w_sem.at[3])
    cache_copies = [
        pltpu.make_async_copy(cache_key, ckey, cache_sem.at[0]),
        pltpu.make_async_copy(cache_value, cvalue, cache_sem.at[1]),
    ]

    def qkv(t, q):
        b = block_of(q, core)
        r0 = b * BLK

        def norm_rows(i, _):
            r = pl.multiple_of(r0 + i * NORM_ROWS, NORM_ROWS)
            wide = state[pl.ds(r, NORM_ROWS), :].astype(F32)
            meansq = jnp.mean(wide * wide, axis=-1, keepdims=True)
            normed[pl.ds(pl.multiple_of(i * NORM_ROWS, NORM_ROWS), NORM_ROWS), :] = (
                wide * lax.rsqrt(meansq + EPS) * gain[...].reshape(1, width)
            ).astype(BF16)
            return 0

        lax.fori_loop(0, BLK // NORM_ROWS, norm_rows, 0)
        for n in range(0, 3 * lw, COLS):
            out = jnp.dot(normed[...], wqkv[:, n : n + COLS], preferred_element_type=F32)
            for c in range(n, min(n + COLS, 3 * lw), HD):
                kind, lane = divmod(c, lw)
                piece = out[:, c - n : c - n + HD].astype(BF16)
                if kind == 2:
                    queries[lane // HD, pl.ds(pl.multiple_of(r0, BLK), BLK), :] = piece
                    continue
                kv[t][HALO + b, kind, lane // HD] = piece

    def temporal(t, r, h):
        lanes = slice(h * HD, (h + 1) * HD)
        at = pl.ds(r, TIME_ROWS)
        query = queries[h, at, :].astype(F32)
        b = lax.div(r, BLK)
        inner = pl.ds(pl.multiple_of(lax.rem(r, BLK), TIME_ROWS), TIME_ROWS)
        frames = range(t, FRAMES)
        keys = [ckey[f, at, lanes] for f in frames]
        keys += [kv0[HALO + b, 0, h, inner]] * t
        scores = [jnp.sum(query * k.astype(F32), axis=-1, keepdims=True) for k in keys]
        top = functools.reduce(jnp.maximum, scores)
        exps = [jnp.exp2((s - top) * SCALE2) for s in scores]
        values = [cvalue[f, at, lanes] for f in frames]
        values += [kv0[HALO + b, 1, h, inner]] * t
        acc = functools.reduce(jnp.add, [e * v.astype(F32) for e, v in zip(exps, values)])
        top_t[at, lanes] = jnp.broadcast_to(top, (TIME_ROWS, HD))
        sum_t[at, lanes] = jnp.broadcast_to(functools.reduce(jnp.add, exps), (TIME_ROWS, HD))
        acc_t[at, lanes] = acc

    def temporal_block(t, q):
        r0 = block_of(q, core) * BLK

        def body(i, _):
            r = pl.multiple_of(r0 + i * TIME_ROWS, TIME_ROWS)
            for h in range(heads):
                temporal(t, r, h)
            return 0

        lax.fori_loop(0, BLK // TIME_ROWS, body, 0)

    def attend(t, b):
        r = pl.ds(pl.multiple_of(b * BLK, BLK), BLK)
        live = counts[b]
        where, bias = [], []
        for j in range(MAXK):
            rel = pattern[b, j] - (space * blocks + b) + total_blocks // 2
            rel = jnp.bitwise_and(rel, total_blocks - 1) - total_blocks // 2
            where.append(jnp.clip(HALO + b + rel, 0, window - 1))
            bias.append(jnp.where(j < live, jnp.float32(0.0), jnp.float32(MASKED)))
        tops = []
        for h in range(heads):
            lanes = slice(h * HD, (h + 1) * HD)
            query = queries[h, r, :]
            top = None
            for j in range(0, MAXK, 2):
                pair = jnp.concatenate([kv[t][where[j + i], 0, h] for i in range(2)], axis=0)
                s = lax.dot_general(
                    query, pair, (((1,), (1,)), ((), ())), preferred_element_type=F32
                )
                for i in range(2):
                    slot = s[:, i * BLK : (i + 1) * BLK] + bias[j + i]
                    scores[h, j + i] = slot
                    top = slot if top is None else jnp.maximum(top, slot)
            tops.append(jnp.max(top, axis=-1, keepdims=True))
        for h in range(heads):
            lanes = slice(h * HD, (h + 1) * HD)
            old = top_t[r, lanes]
            top = jnp.maximum(old, jnp.broadcast_to(tops[h], (BLK, HD)))
            keep = jnp.exp2((old - top) * SCALE2)
            total = None
            for j in range(MAXK):
                e = jnp.exp2((scores[h, j] - top) * SCALE2)
                weights[h, j] = e.astype(BF16)
                total = e if total is None else total + e
            total = sum_t[r, lanes] * keep + jnp.sum(total, axis=-1, keepdims=True)
            values = jnp.concatenate([kv[t][where[j], 1, h] for j in range(MAXK)], axis=0)
            probs = jnp.concatenate([weights[h, j] for j in range(MAXK)], axis=1)
            mixed = jnp.dot(probs, values, preferred_element_type=F32)
            att[t, z * heads + h, r, :] = ((acc_t[r, lanes] * keep + mixed) / total).astype(BF16)

    def update(t, q):
        r = pl.ds(pl.multiple_of(block_of(q, core) * BLK, BLK), BLK)
        mixed = jnp.concatenate([att[t, i, r, :] for i in range(width // HD)], axis=1)
        for n in range(0, width, COLS):
            u = jnp.dot(mixed, wout[:, n : n + COLS], preferred_element_type=F32)
            state[r, n : n + COLS] = (state[r, n : n + COLS].astype(F32) + u).astype(BF16)

    for q in reversed(range(blocks)):
        in_copy(q).start()
    for copy in weight_copies:
        copy.start()
    w_out_copy.start()

    barrier = pltpu.get_barrier_semaphore()
    for dev in (up, down, partner, near_dev, far_dev, far_src):
        pl.semaphore_signal(barrier, inc=1, device_id=dev, device_id_type=MESH)
    pl.semaphore_wait(barrier, 6)

    for copy in weight_copies:
        copy.wait()
    w_out_copy.wait()
    for d in range(2):
        w_copy(d).start()
    for copy in cache_copies:
        copy.start()

    def first_qkv(i, _):
        q = blocks - 1 - i
        in_copy(q).wait()
        qkv(0, q)
        near_start(0, q)
        chip_copy(0, q).start()
        return 0

    lax.fori_loop(0, blocks, first_qkv, 0)
    for copy in cache_copies:
        copy.wait()

    def near_wait(t, q):
        near_copy(t, q).wait_recv()
        relay_copy(t, q).start()

    early = (5, 1)

    def first_temporal(q, _):
        temporal_block(0, q)

        @pl.when(q > 0)
        def _():
            near_wait(0, blocks - q)

        return 0

    lax.fori_loop(0, early[0], first_temporal, 0)

    def forward(t, q):
        for d in range(2):
            gather_copy(t, q, d).wait_recv()
            forward_copy(t, q, d).start()

    def land_near(t, q):
        near_copy(t, q, True).wait_recv()
        kv[t][near_window(q)] = late[t, NEAR_LATE - 1 - q]

    def land_far(t, q):
        far_copy(t, q).wait_recv()
        kv[t][28 * core + block_of(q, core) - FAR * (1 - core)] = late[t, NEAR_LATE + q]

    for t in range(STEPS):
        last = t + 1 == STEPS
        if t == 0:
            near_copy(t, 3).wait_recv()
            far_copy(t, 0).start()
            for d in range(2):
                w_copy(d).wait_recv()
                w_forward(d).start()
            w_chip(0).start()
            w_chip(2).start()
        else:
            near_copy(t, 3).wait_recv()
            for q in (4, 5, 6):
                near_wait(t, q)
            temporal_block(t, 0)
            near_wait(t, 7)
            far_copy(t, 2).start()
            far_copy(t, 3).start()
        for q in range(blocks):
            chip_copy(t, q).wait_recv()
        for q in range(FAR, blocks):
            relay_copy(t, q).wait_recv()

        def tick(i, _, t=t, last=last):
            @pl.when(i < blocks)
            def _():
                @pl.when((i > 0) & (i <= NEAR_LATE))
                def _():
                    land_near(t, NEAR_LATE - i)
                    if t == 0:
                        far_copy(t, i).start()

                @pl.when(i > NEAR_LATE)
                def _():
                    land_far(t, i - NEAR_LATE - 1)

                attend(t, block_of(i, core))
                for d in range(2):
                    gather_copy(t, i, d).start()

            @pl.when((i >= FORWARD_LAG[t]) & (i < blocks + FORWARD_LAG[t]))
            def _():
                forward(t, i - FORWARD_LAG[t])

            @pl.when(i < blocks - early[t])
            def _():
                temporal_block(t, i + early[t])

            if t == 0:

                @pl.when(i == FINISH_LAG[t])
                def _():
                    for d in range(2):
                        w_forward(d).wait_recv()
                    w_chip(1).start()
                    for k in range(3):
                        w_chip(k).wait_recv()

            @pl.when(i >= FINISH_LAG[t])
            def _():
                q = i - FINISH_LAG[t]
                for d in range(2):
                    forward_copy(t, q, d).wait_recv()
                update(t, q)
                if not last:
                    qkv(t + 1, q)
                    near_start(t + 1, q)
                    chip_copy(t + 1, q).start()

                    @pl.when(q < 2)
                    def _():
                        far_copy(t + 1, q).start()

            return 0

        lax.fori_loop(0, blocks + FINISH_LAG[t], tick, 0)

    for t in range(STEPS):

        def drain(q, _, t=t):
            @pl.when(q < NEAR_LATE)
            def _():
                near_copy(t, q, True).wait_send()

            @pl.when(q >= NEAR_LATE)
            def _():
                near_copy(t, q).wait_send()

            chip_copy(t, q).wait_send()
            for d in range(2):
                gather_copy(t, q, d).wait_send()
                forward_copy(t, q, d).wait_send()

            @pl.when(q < FAR)
            def _():
                far_copy(t, q).wait_send()

            @pl.when(q >= FAR)
            def _():
                relay_copy(t, q).wait_send()

            return 0

        lax.fori_loop(0, blocks, drain, 0)
    for d in range(2):
        w_copy(d).wait_send()
        w_forward(d).wait_send()
    for k in range(3):
        w_chip(k).wait_send()


def on_device(
    n_space, n_head,
    snapshot, norm_gain, w_query, w_key, w_value, w_out, cache_key, cache_value, pattern, counts,
):
    rows, width = snapshot.shape
    lw = w_query.shape[1]
    blocks = rows // BLK
    heads = lw // HD
    any_spec = pl.BlockSpec(memory_space=pl.ANY)
    smem = pl.BlockSpec(memory_space=pltpu.SMEM)
    window = blocks + 2 * HALO
    dma = pltpu.SemaphoreType.DMA
    return pl.pallas_call(
        functools.partial(kernel, n_space, n_head),
        out_shape=pltpu.VMEM((rows, width), BF16),
        in_specs=[smem, smem, any_spec, pl.BlockSpec(memory_space=pltpu.VMEM)] + [any_spec] * 6,
        out_specs=pl.BlockSpec(memory_space=pltpu.VMEM),
        scratch_shapes=[
            pltpu.VMEM((width, 3 * lw), BF16),
            pltpu.VMEM((width, width), BF16),
            pltpu.VMEM((FRAMES, rows, lw), BF16),
            pltpu.VMEM((FRAMES, rows, lw), BF16),
            pltpu.VMEM((window, 2, heads, BLK, HD), BF16),
            pltpu.VMEM((window, 2, heads, BLK, HD), BF16),
            pltpu.VMEM((STEPS, NEAR_LATE + FAR, 2, heads, BLK, HD), BF16),
            pltpu.VMEM((STEPS, width // HD, rows, HD), BF16),
            pltpu.VMEM((heads, rows, HD), BF16),
            pltpu.VMEM((BLK, width), BF16),
            pltpu.VMEM((rows, lw), F32),
            pltpu.VMEM((rows, lw), F32),
            pltpu.VMEM((rows, lw), F32),
            pltpu.VMEM((heads, MAXK, BLK, BLK), F32),
            pltpu.VMEM((heads, MAXK, BLK, BLK), BF16),
            dma((blocks,)), dma((4,)), dma((2,)),
            dma((STEPS, blocks)), dma((STEPS, blocks)),
            dma((STEPS, blocks)), dma((STEPS, blocks)),
            dma((STEPS, FAR)), dma((STEPS, FAR)),
            dma((STEPS, FAR)), dma((STEPS, FAR)),
            dma((STEPS, blocks, 2)), dma((STEPS, blocks, 2)),
            dma((STEPS, blocks, 2)), dma((STEPS, blocks, 2)),
            dma((2,)), dma((2,)), dma((2,)), dma((2,)), dma((3,)), dma((3,)),
        ],
        compiler_params=pltpu.CompilerParams(
            collective_id=0, has_side_effects=True, vmem_limit_bytes=56 * 1024 * 1024
        ),
        name="rollout",
    )(
        pattern, counts, snapshot, norm_gain,
        w_query, w_key, w_value, w_out, cache_key, cache_value,
    )


def solution(mesh):
    placed = (
        P("space", None),
        P(),
        P(None, "head"),
        P(None, "head"),
        P(None, "head"),
        P("head", None),
        P(None, "space", "head"),
        P(None, "space", "head"),
        P("space", None),
        P("space"),
    )
    body = functools.partial(on_device, mesh.shape["space"], mesh.shape["head"])
    return jax.shard_map(
        body, mesh=mesh, in_specs=placed, out_specs=P("space", None), check_vma=False
    )
```

```python
import functools
import math

import jax
import jax.numpy as jnp
from jax import lax
from jax.experimental import pallas as pl
from jax.experimental.pallas import tpu as pltpu
from jax.sharding import PartitionSpec as P

HD = 128
BLK = 128
MAXK = 8
FRAMES = 8
STEPS = 2
HALO = 12
FAR = 4
FORWARD_LAG = (2, 2)
FINISH_LAG = (4, 4)
NEAR_LATE = 3
EPS = 1e-05
MASKED = -1e30
MESH = pl.DeviceIdType.MESH
F32 = jnp.float32
BF16 = jnp.bfloat16
SCALE2 = math.log2(math.e) / math.sqrt(HD)
NORM_ROWS = 64
COLS = 512
TIME_ROWS = 32


def kernel(
    n_space, n_head,
    pattern, counts, snapshot, gain, w_query, w_key, w_value, w_out, cache_key, cache_value,
    state,
    wqkv, wout, ckey, cvalue, kv0, kv1, late, att, queries, normed, top_t, sum_t, acc_t, scores, weights,
    in_sem, w_sem, cache_sem,
    near_s, near_r, chip_s, chip_r, far_s, far_r, rel_s, rel_r, ag_s, ag_r, fw_s, fw_r,
    wd_s, wd_r, wf_s, wf_r, wc_s, wc_r,
):
    kv = (kv0, kv1)
    rows, width = state.shape
    lw = w_query.shape[1]
    heads = lw // HD
    blocks = rows // BLK
    total_blocks = blocks * n_space
    window = kv0.shape[0]

    space = lax.axis_index("space")
    z = lax.axis_index("head")
    core = lax.rem(space, 2)

    def wrap(s):
        return lax.rem(s + n_space, n_space)

    up = (space, lax.rem(z + 1, n_head))
    down = (space, lax.rem(z + n_head - 1, n_head))
    partner = (space + 1 - 2 * core, z)
    near_dev = (wrap(space - 1 + 2 * core), z)
    far_dev = (wrap(space + 2 - 4 * core), z)
    far_src = (wrap(space - 2 + 4 * core), z)
    z_up = lax.rem(z + 1, n_head)
    z_down = lax.rem(z + n_head - 1, n_head)

    def block_of(q, c):
        return (1 - c) * (blocks - 1 - q) + c * q

    def rcopy(src, dst, ssem, rsem, dev):
        return pltpu.make_async_remote_copy(
            src_ref=src, dst_ref=dst, send_sem=ssem, recv_sem=rsem, device_id=dev, device_id_type=MESH
        )

    def near_window(q):
        return 4 + 16 * core + block_of(q, 1 - core)

    def near_copy(t, q, last=False):
        b = block_of(q, core)
        return rcopy(
            kv[t].at[HALO + b],
            late.at[t, NEAR_LATE - 1 - q] if last else kv[t].at[20 - 16 * core + b],
            near_s.at[t, q], near_r.at[t, q], near_dev,
        )

    def near_start(t, q):
        @pl.when(q < NEAR_LATE)
        def _():
            near_copy(t, q, True).start()

        @pl.when(q >= NEAR_LATE)
        def _():
            near_copy(t, q).start()

    def chip_copy(t, q):
        b = block_of(q, core)
        return rcopy(
            kv[t].at[HALO + b],
            kv[t].at[4 + 16 * core + b],
            chip_s.at[t, q], chip_r.at[t, q], partner,
        )

    def far_copy(t, q):
        b = block_of(q, core)
        return rcopy(
            kv[t].at[HALO + b],
            late.at[t, NEAR_LATE + q],
            far_s.at[t, q], far_r.at[t, q], far_dev,
        )

    def relay_copy(t, q):
        w = near_window(q)
        return rcopy(
            kv[t].at[w],
            kv[t].at[w - 8 + 16 * core],
            rel_s.at[t, q - FAR], rel_r.at[t, q - FAR], partner,
        )

    def gather_copy(t, q, d):
        r = pl.multiple_of(block_of(q, core) * BLK, BLK)
        part = att.at[t, pl.ds(z * heads, heads), pl.ds(r, BLK), :]
        return rcopy(part, part, ag_s.at[t, q, d], ag_r.at[t, q, d], up if d == 0 else down)

    def forward_copy(t, q, d):
        r = pl.multiple_of(block_of(q, core) * BLK + d * (BLK // 2), BLK // 2)
        source = z_down if d == 0 else z_up
        part = att.at[t, pl.ds(source * heads, heads), pl.ds(r, BLK // 2), :]
        return rcopy(part, part, fw_s.at[t, q, d], fw_r.at[t, q, d], up if d == 0 else down)

    half = lw // 2

    def w_rows(group, offset, count):
        return wout.at[pl.ds(pl.multiple_of(group * lw + offset, 32), count), :]

    def w_copy(d):
        part = w_rows(z, half * core, half)
        return rcopy(part, part, wd_s.at[d], wd_r.at[d], up if d == 0 else down)

    def w_forward(d):
        part = w_rows(z_down if d == 0 else z_up, half * core + d * (half // 2), half // 2)
        return rcopy(part, part, wf_s.at[d], wf_r.at[d], up if d == 0 else down)

    def w_chip(k):
        part = w_rows(lax.rem(z + 1 + k, n_head), half * core, half)
        return rcopy(part, part, wc_s.at[k], wc_r.at[k], partner)

    def in_copy(q):
        r = pl.multiple_of(block_of(q, core) * BLK, BLK)
        return pltpu.make_async_copy(
            snapshot.at[pl.ds(r, BLK), :], state.at[pl.ds(r, BLK), :], in_sem.at[q]
        )

    weight_copies = [
        pltpu.make_async_copy(ref, wqkv.at[:, pl.ds(i * lw, lw)], w_sem.at[i])
        for i, ref in enumerate((w_key, w_value, w_query))
    ]
    w_out_copy = pltpu.make_async_copy(w_out, w_rows(z, 0, lw), w_sem.at[3])
    cache_copies = [
        pltpu.make_async_copy(cache_key, ckey, cache_sem.at[0]),
        pltpu.make_async_copy(cache_value, cvalue, cache_sem.at[1]),
    ]

    def qkv(t, q):
        b = block_of(q, core)
        r0 = b * BLK

        def norm_rows(i, _):
            r = pl.multiple_of(r0 + i * NORM_ROWS, NORM_ROWS)
            wide = state[pl.ds(r, NORM_ROWS), :].astype(F32)
            meansq = jnp.mean(wide * wide, axis=-1, keepdims=True)
            normed[pl.ds(pl.multiple_of(i * NORM_ROWS, NORM_ROWS), NORM_ROWS), :] = (
                wide * lax.rsqrt(meansq + EPS) * gain[...].reshape(1, width)
            ).astype(BF16)
            return 0

        lax.fori_loop(0, BLK // NORM_ROWS, norm_rows, 0)
        for n in range(0, 3 * lw, COLS):
            out = jnp.dot(normed[...], wqkv[:, n : n + COLS], preferred_element_type=F32)
            for c in range(n, min(n + COLS, 3 * lw), HD):
                kind, lane = divmod(c, lw)
                piece = out[:, c - n : c - n + HD].astype(BF16)
                if kind == 2:
                    queries[lane // HD, pl.ds(pl.multiple_of(r0, BLK), BLK), :] = piece
                    continue
                kv[t][HALO + b, kind, lane // HD] = piece

    def temporal(t, r, h):
        lanes = slice(h * HD, (h + 1) * HD)
        at = pl.ds(r, TIME_ROWS)
        query = queries[h, at, :].astype(F32)
        b = lax.div(r, BLK)
        inner = pl.ds(pl.multiple_of(lax.rem(r, BLK), TIME_ROWS), TIME_ROWS)
        frames = range(t, FRAMES)
        keys = [ckey[f, at, lanes] for f in frames]
        keys += [kv0[HALO + b, 0, h, inner]] * t
        scores = [jnp.sum(query * k.astype(F32), axis=-1, keepdims=True) for k in keys]
        top = functools.reduce(jnp.maximum, scores)
        exps = [jnp.exp2((s - top) * SCALE2) for s in scores]
        values = [cvalue[f, at, lanes] for f in frames]
        values += [kv0[HALO + b, 1, h, inner]] * t
        acc = functools.reduce(jnp.add, [e * v.astype(F32) for e, v in zip(exps, values)])
        top_t[at, lanes] = jnp.broadcast_to(top, (TIME_ROWS, HD))
        sum_t[at, lanes] = jnp.broadcast_to(functools.reduce(jnp.add, exps), (TIME_ROWS, HD))
        acc_t[at, lanes] = acc

    def temporal_block(t, q):
        r0 = block_of(q, core) * BLK

        def body(i, _):
            r = pl.multiple_of(r0 + i * TIME_ROWS, TIME_ROWS)
            for h in range(heads):
                temporal(t, r, h)
            return 0

        lax.fori_loop(0, BLK // TIME_ROWS, body, 0)

    def attend(t, b):
        r = pl.ds(pl.multiple_of(b * BLK, BLK), BLK)
        live = counts[b]
        where, bias = [], []
        for j in range(MAXK):
            rel = pattern[b, j] - (space * blocks + b) + total_blocks // 2
            rel = jnp.bitwise_and(rel, total_blocks - 1) - total_blocks // 2
            where.append(jnp.clip(HALO + b + rel, 0, window - 1))
            bias.append(jnp.where(j < live, jnp.float32(0.0), jnp.float32(MASKED)))
        tops = []
        for h in range(heads):
            lanes = slice(h * HD, (h + 1) * HD)
            query = queries[h, r, :]
            top = None
            for j in range(0, MAXK, 2):
                pair = jnp.concatenate([kv[t][where[j + i], 0, h] for i in range(2)], axis=0)
                s = lax.dot_general(
                    query, pair, (((1,), (1,)), ((), ())), preferred_element_type=F32
                )
                for i in range(2):
                    slot = s[:, i * BLK : (i + 1) * BLK] + bias[j + i]
                    scores[h, j + i] = slot
                    top = slot if top is None else jnp.maximum(top, slot)
            tops.append(jnp.max(top, axis=-1, keepdims=True))
        for h in range(heads):
            lanes = slice(h * HD, (h + 1) * HD)
            old = top_t[r, lanes]
            top = jnp.maximum(old, jnp.broadcast_to(tops[h], (BLK, HD)))
            keep = jnp.exp2((old - top) * SCALE2)
            total = None
            for j in range(MAXK):
                e = jnp.exp2((scores[h, j] - top) * SCALE2)
                weights[h, j] = e.astype(BF16)
                total = e if total is None else total + e
            total = sum_t[r, lanes] * keep + jnp.sum(total, axis=-1, keepdims=True)
            values = jnp.concatenate([kv[t][where[j], 1, h] for j in range(MAXK)], axis=0)
            probs = jnp.concatenate([weights[h, j] for j in range(MAXK)], axis=1)
            mixed = jnp.dot(probs, values, preferred_element_type=F32)
            att[t, z * heads + h, r, :] = ((acc_t[r, lanes] * keep + mixed) / total).astype(BF16)

    def update(t, q):
        r = pl.ds(pl.multiple_of(block_of(q, core) * BLK, BLK), BLK)
        mixed = jnp.concatenate([att[t, i, r, :] for i in range(width // HD)], axis=1)
        for n in range(0, width, COLS):
            u = jnp.dot(mixed, wout[:, n : n + COLS], preferred_element_type=F32)
            state[r, n : n + COLS] = (state[r, n : n + COLS].astype(F32) + u).astype(BF16)

    for q in reversed(range(blocks)):
        in_copy(q).start()
    for copy in weight_copies:
        copy.start()
    w_out_copy.start()

    barrier = pltpu.get_barrier_semaphore()
    for dev in (up, down, partner, near_dev, far_dev, far_src):
        pl.semaphore_signal(barrier, inc=1, device_id=dev, device_id_type=MESH)
    pl.semaphore_wait(barrier, 6)

    for copy in weight_copies:
        copy.wait()
    w_out_copy.wait()
    for d in range(2):
        w_copy(d).start()
    for copy in cache_copies:
        copy.start()

    def first_qkv(i, _):
        q = blocks - 1 - i
        in_copy(q).wait()
        qkv(0, q)
        near_start(0, q)
        chip_copy(0, q).start()
        return 0

    lax.fori_loop(0, blocks, first_qkv, 0)
    for copy in cache_copies:
        copy.wait()

    def near_wait(t, q):
        near_copy(t, q).wait_recv()
        relay_copy(t, q).start()

    early = (5, 1)

    def first_temporal(q, _):
        temporal_block(0, q)

        @pl.when(q > 0)
        def _():
            near_wait(0, blocks - q)

        return 0

    lax.fori_loop(0, early[0], first_temporal, 0)

    def forward(t, q):
        for d in range(2):
            gather_copy(t, q, d).wait_recv()
            forward_copy(t, q, d).start()

    def land_near(t, q):
        near_copy(t, q, True).wait_recv()
        kv[t][near_window(q)] = late[t, NEAR_LATE - 1 - q]

    def land_far(t, q):
        far_copy(t, q).wait_recv()
        kv[t][28 * core + block_of(q, core) - FAR * (1 - core)] = late[t, NEAR_LATE + q]

    for t in range(STEPS):
        last = t + 1 == STEPS
        if t == 0:
            near_copy(t, 3).wait_recv()
            far_copy(t, 0).start()
            for d in range(2):
                w_copy(d).wait_recv()
                w_forward(d).start()
            w_chip(0).start()
            w_chip(2).start()
        else:
            near_copy(t, 3).wait_recv()
            for q in (4, 5, 6):
                near_wait(t, q)
            temporal_block(t, 0)
            near_wait(t, 7)
            for q in range(FAR):
                far_copy(t, q).start()
        for q in range(blocks):
            chip_copy(t, q).wait_recv()
        for q in range(FAR, blocks):
            relay_copy(t, q).wait_recv()

        def tick(i, _, t=t, last=last):
            @pl.when(i < blocks)
            def _():
                @pl.when((i > 0) & (i <= NEAR_LATE))
                def _():
                    land_near(t, NEAR_LATE - i)
                    if t == 0:
                        far_copy(t, i).start()

                @pl.when(i > NEAR_LATE)
                def _():
                    land_far(t, i - NEAR_LATE - 1)

                attend(t, block_of(i, core))
                for d in range(2):
                    gather_copy(t, i, d).start()

            @pl.when((i >= FORWARD_LAG[t]) & (i < blocks + FORWARD_LAG[t]))
            def _():
                forward(t, i - FORWARD_LAG[t])

            @pl.when(i < blocks - early[t])
            def _():
                temporal_block(t, i + early[t])

            if t == 0:

                @pl.when(i == FINISH_LAG[t])
                def _():
                    for d in range(2):
                        w_forward(d).wait_recv()
                    w_chip(1).start()
                    for k in range(3):
                        w_chip(k).wait_recv()

            @pl.when(i >= FINISH_LAG[t])
            def _():
                q = i - FINISH_LAG[t]
                for d in range(2):
                    forward_copy(t, q, d).wait_recv()
                update(t, q)
                if not last:
                    qkv(t + 1, q)
                    near_start(t + 1, q)
                    chip_copy(t + 1, q).start()

            return 0

        lax.fori_loop(0, blocks + FINISH_LAG[t], tick, 0)

    for t in range(STEPS):

        def drain(q, _, t=t):
            @pl.when(q < NEAR_LATE)
            def _():
                near_copy(t, q, True).wait_send()

            @pl.when(q >= NEAR_LATE)
            def _():
                near_copy(t, q).wait_send()

            chip_copy(t, q).wait_send()
            for d in range(2):
                gather_copy(t, q, d).wait_send()
                forward_copy(t, q, d).wait_send()

            @pl.when(q < FAR)
            def _():
                far_copy(t, q).wait_send()

            @pl.when(q >= FAR)
            def _():
                relay_copy(t, q).wait_send()

            return 0

        lax.fori_loop(0, blocks, drain, 0)
    for d in range(2):
        w_copy(d).wait_send()
        w_forward(d).wait_send()
    for k in range(3):
        w_chip(k).wait_send()


def on_device(
    n_space, n_head,
    snapshot, norm_gain, w_query, w_key, w_value, w_out, cache_key, cache_value, pattern, counts,
):
    rows, width = snapshot.shape
    lw = w_query.shape[1]
    blocks = rows // BLK
    heads = lw // HD
    any_spec = pl.BlockSpec(memory_space=pl.ANY)
    smem = pl.BlockSpec(memory_space=pltpu.SMEM)
    window = blocks + 2 * HALO
    dma = pltpu.SemaphoreType.DMA
    return pl.pallas_call(
        functools.partial(kernel, n_space, n_head),
        out_shape=pltpu.VMEM((rows, width), BF16),
        in_specs=[smem, smem, any_spec, pl.BlockSpec(memory_space=pltpu.VMEM)] + [any_spec] * 6,
        out_specs=pl.BlockSpec(memory_space=pltpu.VMEM),
        scratch_shapes=[
            pltpu.VMEM((width, 3 * lw), BF16),
            pltpu.VMEM((width, width), BF16),
            pltpu.VMEM((FRAMES, rows, lw), BF16),
            pltpu.VMEM((FRAMES, rows, lw), BF16),
            pltpu.VMEM((window, 2, heads, BLK, HD), BF16),
            pltpu.VMEM((window, 2, heads, BLK, HD), BF16),
            pltpu.VMEM((STEPS, NEAR_LATE + FAR, 2, heads, BLK, HD), BF16),
            pltpu.VMEM((STEPS, width // HD, rows, HD), BF16),
            pltpu.VMEM((heads, rows, HD), BF16),
            pltpu.VMEM((BLK, width), BF16),
            pltpu.VMEM((rows, lw), F32),
            pltpu.VMEM((rows, lw), F32),
            pltpu.VMEM((rows, lw), F32),
            pltpu.VMEM((heads, MAXK, BLK, BLK), F32),
            pltpu.VMEM((heads, MAXK, BLK, BLK), BF16),
            dma((blocks,)), dma((4,)), dma((2,)),
            dma((STEPS, blocks)), dma((STEPS, blocks)),
            dma((STEPS, blocks)), dma((STEPS, blocks)),
            dma((STEPS, FAR)), dma((STEPS, FAR)),
            dma((STEPS, FAR)), dma((STEPS, FAR)),
            dma((STEPS, blocks, 2)), dma((STEPS, blocks, 2)),
            dma((STEPS, blocks, 2)), dma((STEPS, blocks, 2)),
            dma((2,)), dma((2,)), dma((2,)), dma((2,)), dma((3,)), dma((3,)),
        ],
        compiler_params=pltpu.CompilerParams(
            collective_id=0, has_side_effects=True, vmem_limit_bytes=56 * 1024 * 1024
        ),
        name="rollout",
    )(
        pattern, counts, snapshot, norm_gain,
        w_query, w_key, w_value, w_out, cache_key, cache_value,
    )


def solution(mesh):
    placed = (
        P("space", None),
        P(),
        P(None, "head"),
        P(None, "head"),
        P(None, "head"),
        P("head", None),
        P(None, "space", "head"),
        P(None, "space", "head"),
        P("space", None),
        P("space"),
    )
    body = functools.partial(on_device, mesh.shape["space"], mesh.shape["head"])
    return jax.shard_map(
        body, mesh=mesh, in_specs=placed, out_specs=P("space", None), check_vma=False
    )
```
